32 devices in a mesh: group: 2 (over y), replica: 4 (over z), seq: 4 (over x, core).
Axes of the slice: x: 2, y: 2, z: 4, core: 2. Of those that a mesh axis runs over, the one named last changes fastest.
Arguments:
- features: bfloat16 [16, 2048, 1152], P(('group', 'replica'), 'seq'), may hold values from -6 to 6
- condition: bfloat16 [16, 1152], P(('group', 'replica')), may hold values from -6 to 6
- modulator: bfloat16 [1152, 6912], P('group'), may hold values from -0.1875 to 0.1875
- modulator_bias: bfloat16 [6912], P('group'), may hold values from -3 to 3
- projector: bfloat16 [1152, 3456], P('group'), may hold values from -0.1875 to 0.1875
- projector_bias: bfloat16 [2304], P('group'), may hold values from -0.29882812 to 0.29882812
- combiner: bfloat16 [1152, 1152], P('group'), may hold values from -3 to 3
- combiner_bias: bfloat16 [1152], P('group'), may hold values from -3 to 3
- expander: bfloat16 [1152, 4608], P('group'), may hold values from -0.1875 to 0.1875
- expander_bias: bfloat16 [4608], P('group'), may hold values from -3 to 3
- reducer: bfloat16 [4608, 1152], P('group'), may hold values from -0.09375 to 0.09375
- reducer_bias: bfloat16 [1152], P('group'), may hold values from -3 to 3
- cotangent: bfloat16 [16, 2048, 1152], P(('group', 'replica'), 'seq'), may hold values from -6 to 6
Outputs:
- block_output: bfloat16 [16, 2048, 1152], P(('group', 'replica'), 'seq')
- features_grad: float32 [16, 2048, 1152], P(('group', 'replica'), 'seq')
- condition_grad: float32 [16, 1152], P(('group', 'replica'))
- modulator_grad: float32 [1152, 6912], P('group')
- modulator_bias_grad: float32 [6912], P('group')
- projector_grad: float32 [1152, 3456], P('group')
- projector_bias_grad: float32 [2304], P('group')
- combiner_grad: float32 [1152, 1152], P('group')
- combiner_bias_grad: float32 [1152], P('group')
- expander_grad: float32 [1152, 4608], P('group')
- expander_bias_grad: float32 [4608], P('group')
- reducer_grad: float32 [4608, 1152], P('group')
- reducer_bias_grad: float32 [1152], P('group')
The draws below stay inside these ranges and needn't reach their ends.
All inputs are finite; a program needn't handle non-finite values.
Results may differ from the reference program's by a relative error of at most 0.018.
Values may be sent and summed in bfloat16 or wider, within the bound.
No kernel may reach another device: no remote copies, remote signals or barrier semaphores. Data moves between devices by JAX's collectives and lax.ppermute only.
A program may use at most 448 MiB of HBM per device.

```python
import jax
import jax.numpy as jnp
from jax import lax

D = 1152
HEADS = 16
HEAD_DIM = 72
FF = 4608
LAT_DEV = 2
SEQ_LEN = 2048
LATENTS = 16


def shard_levels(stream_key, extent, split, smallest, largest):
    gain = 1.0
    for dim, shards_of in split:
        heights = jax.random.uniform(jax.random.fold_in(jax.random.fold_in(stream_key, 6), dim), (shards_of,), jnp.float32, smallest / len(split), largest / len(split))
        gain = gain * jnp.repeat(jnp.exp(heights), extent[dim] // shards_of).reshape((-1,) + (1,) * (len(extent) - 1 - dim))
    return gain


def bell_draw(key, extent, deviation, most, cuts=(), kind=jnp.bfloat16):
    level = shard_levels(key, extent, cuts, -0.22, 0.18) if cuts else 1.0
    drawn = jax.random.normal(key, extent, jnp.float32) * deviation * level
    return jnp.minimum(jnp.maximum(drawn, -most), most).astype(kind)


def setup_inputs(seed: int = 0) -> dict:
    key_of = jax.random.split(jax.random.key(seed), 14)
    return {
        "features": bell_draw(key_of[0], (LATENTS, SEQ_LEN, D), 1.0, 6.0, ((0, 8), (1, 4))),
        "condition": bell_draw(key_of[1], (LATENTS, D), 1.0, 6.0, ((0, 8),)),
        "modulator": bell_draw(key_of[2], (D, 6 * D), D ** -0.5, 0.1875, ((0, 2),)),
        "modulator_bias": bell_draw(key_of[3], (6 * D,), 0.5, 3.0, ((0, 2),)),
        "projector": bell_draw(key_of[4], (D, 3 * D), D ** -0.5, 0.1875, ((0, 2),)),
        "projector_bias": bell_draw(key_of[5], (2 * D,), 0.05, 0.29882812, ((0, 2),)),
        "combiner": bell_draw(key_of[6], (D, D), 4 ** -0.5, 3.0, ((0, 2),)),
        "combiner_bias": bell_draw(key_of[7], (D,), 0.5, 3.0, ((0, 2),)),
        "expander": bell_draw(key_of[8], (D, FF), D ** -0.5, 0.1875, ((0, 2),)),
        "expander_bias": bell_draw(key_of[9], (FF,), 0.5, 3.0, ((0, 2),)),
        "reducer": bell_draw(key_of[10], (FF, D), FF ** -0.5, 0.09375, ((0, 2),)),
        "reducer_bias": bell_draw(key_of[11], (D,), 0.5, 3.0, ((0, 2),)),
        "cotangent": bell_draw(key_of[12], (LATENTS, SEQ_LEN, D), 1.0, 6.0, ((0, 8), (1, 4))),
    }


@jax.custom_vjp
def low(v):
    return lax.optimization_barrier(v.astype(jnp.bfloat16)).astype(jnp.float32)

@jax.custom_vjp
def low_back(v):
    return v

def low_keep(v):
    return (low(v), None)

def low_pass(kept, grad):
    return (grad,)

def back_keep(v):
    return (v, None)

def back_low(kept, grad):
    return (low(grad),)
low.defvjp(low_keep, low_pass)
low_back.defvjp(back_keep, back_low)

def product(operand, matrix):
    return jnp.einsum('...d,de->...e', operand, matrix, precision=lax.Precision.HIGHEST)

def layer_norm(values):
    centre = lax.optimization_barrier(jnp.mean(values, -1, keepdims=True))
    centred = values - centre
    return centred * lax.rsqrt(lax.optimization_barrier(jnp.mean(centred * centred, -1, keepdims=True)) + 1e-06)

def attend(packed):
    queries, keys_in, values_in = packed
    scores = jnp.einsum('qhd,khd->hqk', queries, keys_in, precision=lax.Precision.HIGHEST) * HEAD_DIM ** (-0.5)
    scores = low_back(scores)
    probabilities = low(jax.nn.softmax(scores, axis=-1))
    context = jnp.einsum('hqk,khd->qhd', probabilities, values_in, precision=lax.Precision.HIGHEST)
    return context.reshape(context.shape[0], HEADS * HEAD_DIM)

def layer(features, condition, modulator, modulator_bias, projector, projector_bias, combiner, combiner_bias, expander, expander_bias, reducer, reducer_bias):
    model_width = features.shape[-1]
    batch_count = features.shape[0]
    length = features.shape[1]
    silu_low = low(jax.nn.silu(condition))
    modulation = low_back(product(silu_low, modulator) + modulator_bias)
    pieces = [modulation[:, None, position * model_width:(position + 1) * model_width] for position in range(6)]
    shift_attn, scale_attn, gate_attn, shift_mlp, scale_mlp, gate_mlp = pieces
    attn_in = low(layer_norm(features) * (1.0 + scale_attn) + shift_attn)
    qkv_bias = jnp.concatenate([projector_bias[:model_width], jnp.zeros((model_width,), jnp.float32), projector_bias[model_width:]])
    qkv = low(low_back(product(attn_in, projector) + qkv_bias))

    def split_heads(tensor):
        return tensor.reshape(batch_count, length, HEADS, HEAD_DIM)
    queries = split_heads(qkv[..., :model_width])
    keys_in = split_heads(qkv[..., model_width:2 * model_width])
    values_in = split_heads(qkv[..., 2 * model_width:])
    context = lax.map(jax.checkpoint(attend), (queries, keys_in, values_in))
    context = low(low_back(context))
    attn_out = low_back(product(context, combiner) + combiner_bias)
    hidden = features + gate_attn * attn_out
    mlp_in = low(layer_norm(hidden) * (1.0 + scale_mlp) + shift_mlp)
    expanded = low_back(product(mlp_in, expander) + expander_bias)
    activated = low(jax.nn.gelu(expanded, approximate=True))
    reduced = low_back(product(activated, reducer) + reducer_bias)
    return hidden + gate_mlp * reduced

def reference(features, condition, modulator, modulator_bias, projector, projector_bias, combiner, combiner_bias, expander, expander_bias, reducer, reducer_bias, cotangent):
    params = tuple((weight_item.astype(jnp.float32) for weight_item in (modulator, modulator_bias, projector, projector_bias, combiner, combiner_bias, expander, expander_bias, reducer, reducer_bias)))
    length = features.shape[1]
    model_width = features.shape[2]
    feature_batches = features.astype(jnp.float32).reshape(-1, LAT_DEV, length, model_width)
    cond_batches = condition.astype(jnp.float32).reshape(-1, LAT_DEV, model_width)
    grad_batches = cotangent.astype(jnp.float32).reshape(-1, LAT_DEV, length, model_width)

    def advance(carried, batch_item):
        latents, conditions, cotangents = batch_item
        result, pullback = jax.vjp(layer, latents, conditions, *params)
        gradients = pullback(cotangents)
        carried = tuple((kept_grad + new_grad for kept_grad, new_grad in zip(carried, gradients[2:])))
        return (carried, (result.astype(jnp.bfloat16), gradients[0], gradients[1]))
    zeros_start = tuple((jnp.zeros_like(weight_item) for weight_item in params))
    totals, (outputs, input_grads, cond_grads) = lax.scan(advance, zeros_start, (feature_batches, cond_batches, grad_batches))
    return (outputs.reshape(features.shape), input_grads.reshape(features.shape), cond_grads.reshape(condition.shape), totals[0], totals[1], totals[2], totals[3], totals[4], totals[5], totals[6], totals[7], totals[8], totals[9])
```

```python
from functools import partial

import jax
import jax.numpy as jnp
from jax import lax
from jax.experimental import pallas as pl
from jax.experimental.pallas import tpu as pltpu
from jax.sharding import PartitionSpec as P

HEADS = 16
HEAD_DIM = 72
SCALE = HEAD_DIM**-0.5
LOW = jnp.bfloat16
F32 = jnp.float32


def contract(left, right, left_dim, right_dim):
    return lax.dot_general(
        left, right, (((left_dim,), (right_dim,)), ((), ())), preferred_element_type=F32
    )


def attend_kernel(count, width, *refs):
    pieces = refs[:count]
    context_ref, exp_ref, inverse_ref = refs[count : count + 3]
    keys, values = refs[count + 3 :]
    step = pl.program_id(1)

    @pl.when(step == 0)
    def _():
        for piece in range(count):
            span = slice(piece * width, (piece + 1) * width)
            keys[span, :] = pieces[piece][1, 0].T
            values[:, span] = pieces[piece][2, 0]

    def one(piece):
        scores = contract(keys[...], pieces[piece][0, 0], 1, 0) * F32(SCALE)
        exponent = jnp.exp(scores - jnp.max(scores, 0, keepdims=True))
        inverse = 1.0 / jnp.sum(exponent, 0, keepdims=True)
        low = exponent.astype(LOW)
        context = contract(values[...], low, 1, 0)
        context_ref[0, 0] = (context * inverse).astype(LOW)
        inverse_ref[0, 0] = inverse
        exp_ref[0, 0] = low

    for piece in range(count):
        pl.when(step == piece)(partial(one, piece))


def attend(pieces):
    count = len(pieces)
    _, heads, dim, width = pieces[0].shape
    total = count * width
    return pl.pallas_call(
        partial(attend_kernel, count, width),
        grid=(heads, count),
        in_specs=[pl.BlockSpec((3, 1, dim, width), lambda h, j: (0, h, 0, 0))] * count,
        out_specs=[
            pl.BlockSpec((1, 1, dim, width), lambda h, j: (j, h, 0, 0)),
            pl.BlockSpec((1, 1, total, width), lambda h, j: (h, j, 0, 0)),
            pl.BlockSpec((1, 1, 1, width), lambda h, j: (h, j, 0, 0)),
        ],
        out_shape=[
            jax.ShapeDtypeStruct((count, heads, dim, width), LOW),
            jax.ShapeDtypeStruct((heads, count, total, width), LOW),
            jax.ShapeDtypeStruct((heads, count, 1, width), F32),
        ],
        scratch_shapes=[pltpu.VMEM((total, dim), LOW), pltpu.VMEM((dim, total), LOW)],
        compiler_params=pltpu.CompilerParams(vmem_limit_bytes=48 << 20),
        name="attend",
    )(*pieces)


KEY_SPAN = 1024


def attend_back_kernel(count, width, *refs):
    pieces = refs[:count]
    grads = refs[count : 2 * count]
    context_ref, exp_ref, inverse_ref, out_ref = refs[2 * count : 2 * count + 4]
    values, keys, key_sum, value_sum = refs[2 * count + 4 :]
    step = pl.program_id(1)
    total = count * width

    @pl.when(step == 0)
    def _():
        for piece in range(count):
            span = slice(piece * width, (piece + 1) * width)
            values[span, :] = pieces[piece][2, 0].T
            keys[:, span] = pieces[piece][1, 0]
        key_sum[...] = jnp.zeros_like(key_sum)
        value_sum[...] = jnp.zeros_like(value_sum)

    def one(piece):
        query = pieces[piece][0, 0]
        grad = (grads[piece][0].astype(F32) * inverse_ref[0, 0]).astype(LOW)
        row_dot = jnp.sum(grad.astype(F32) * context_ref[0, 0].astype(F32), 0, keepdims=True)
        query_grad = jnp.zeros(query.shape, F32)
        for start in range(0, total, KEY_SPAN):
            span = slice(start, start + KEY_SPAN)
            exponent = exp_ref[0, 0, span, :]
            probs_grad = contract(values[span, :], grad, 1, 0)
            scores_grad = (exponent.astype(F32) * (probs_grad - row_dot)).astype(LOW)
            query_grad += contract(keys[:, span], scores_grad, 1, 0)
            value_sum[:, span] += contract(grad, exponent, 1, 1)
            key_sum[:, span] += contract(query, scores_grad, 1, 1)
        out_ref[piece, 0, 0] = (query_grad * F32(SCALE)).astype(LOW)

    for piece in range(count):
        pl.when(step == piece)(partial(one, piece))

    @pl.when(step == count - 1)
    def _():
        for piece in range(count):
            span = slice(piece * width, (piece + 1) * width)
            out_ref[piece, 1, 0] = (key_sum[:, span] * F32(SCALE)).astype(LOW)
            out_ref[piece, 2, 0] = value_sum[:, span].astype(LOW)


def attend_back(pieces, grads, context, exponent, inverse):
    count = len(pieces)
    _, heads, dim, width = pieces[0].shape
    total = count * width
    return pl.pallas_call(
        partial(attend_back_kernel, count, width),
        grid=(heads, count),
        in_specs=[pl.BlockSpec((3, 1, dim, width), lambda h, j: (0, h, 0, 0))] * count
        + [pl.BlockSpec((1, dim, width), lambda h, j: (h, 0, 0))] * count
        + [
            pl.BlockSpec((1, 1, dim, width), lambda h, j: (j, h, 0, 0)),
            pl.BlockSpec((1, 1, total, width), lambda h, j: (h, j, 0, 0)),
            pl.BlockSpec((1, 1, 1, width), lambda h, j: (h, j, 0, 0)),
        ],
        out_specs=pl.BlockSpec((count, 3, 1, dim, width), lambda h, j: (0, 0, h, 0, 0)),
        out_shape=jax.ShapeDtypeStruct((count, 3, heads, dim, width), LOW),
        scratch_shapes=[
            pltpu.VMEM((total, dim), LOW),
            pltpu.VMEM((dim, total), LOW),
            pltpu.VMEM((dim, total), F32),
            pltpu.VMEM((dim, total), F32),
        ],
        compiler_params=pltpu.CompilerParams(vmem_limit_bytes=48 << 20),
        name="attend_back",
    )(*pieces, *grads, context, exponent, inverse)


def swap(value, axis, size, distance):
    return lax.ppermute(value, axis, [(index, index ^ distance) for index in range(size)])


def pick(array, index, axis=0):
    return lax.dynamic_index_in_dim(array, index, axis, keepdims=False)


def put(parts, me):
    full = jnp.zeros((len(parts),) + parts[0].shape, parts[0].dtype)
    for distance, part in enumerate(parts):
        full = lax.dynamic_update_slice_in_dim(full, part[None], me ^ distance, 0)
    return full


def exchange(chunks, size):
    return [chunks[0]] + [swap(chunks[k], "seq", size, k) for k in range(1, size)]


def add_low(one, other):
    return (one.astype(F32) + other.astype(F32)).astype(LOW)


def reduce_shards(grad, sizes):
    groups, replicas, seqs = sizes
    rows, cols = grad.shape
    low = grad.astype(LOW)
    if groups == 2 and seqs == 4 and replicas == 4:
        seq = lax.axis_index("seq")
        near, far = seq & 1, seq >> 1
        group = lax.axis_index("group")
        rep = lax.axis_index("replica")
        view = low.reshape(2, 2, rows // 4, cols)
        own = add_low(pick(view, near, 1), swap(pick(view, 1 - near, 1), "seq", 4, 1))
        own = add_low(pick(own, group), swap(pick(own, 1 - group), "group", 2, 1))
        own = own.reshape(2, rows // 8, cols)
        own = add_low(pick(own, far), swap(pick(own, 1 - far), "seq", 4, 2))
        own = own.reshape(2, rows // 16, cols)
        own = add_low(pick(own, rep >> 1), swap(pick(own, 1 - (rep >> 1)), "replica", 4, 2))
        own = own.reshape(2, rows // 32, cols)
        own = add_low(pick(own, rep & 1), swap(pick(own, 1 - (rep & 1)), "replica", 4, 1))
        full = lax.all_gather(own, "replica", axis=0, tiled=True)
        full = lax.all_gather(full, "seq", axis=0)
        full = full.reshape(2, 2, rows // 8, cols).transpose(1, 0, 2, 3)
        return full.reshape(rows // 2, cols).astype(F32)
    part = lax.psum_scatter(low, "group", scatter_dimension=0, tiled=True)
    return lax.psum(part, ("replica", "seq")).astype(F32)


def normalize(values):
    centre = jnp.mean(values, -1, keepdims=True)
    centred = values - centre
    inverse = lax.rsqrt(jnp.mean(centred * centred, -1, keepdims=True) + 1e-06)
    return (centred * inverse, inverse)


def normalize_back(grad_in, normed, inverse):
    return (
        grad_in
        - jnp.mean(grad_in, -1, keepdims=True)
        - normed * jnp.mean(grad_in * normed, -1, keepdims=True)
    ) * inverse


def matmul(operand, matrix):
    return jnp.einsum("btd,de->bte", operand, matrix, preferred_element_type=F32)


def matmul_back(operand, matrix):
    return jnp.einsum("bte,de->btd", operand, matrix, preferred_element_type=F32)


def outer_sum(operand, other):
    return jnp.einsum("btd,bte->de", operand, other, preferred_element_type=F32)


def body(
    sizes,
    features,
    condition,
    modulator,
    modulator_bias,
    projector,
    projector_bias,
    combiner,
    combiner_bias,
    expander,
    expander_bias,
    reducer,
    reducer_bias,
    cotangent,
):
    groups, replicas, seqs = sizes
    group = lax.axis_index("group")
    rep = lax.axis_index("replica")
    seq = lax.axis_index("seq")
    latents, width, model = features.shape
    rows = modulator.shape[0]
    heads = HEADS // seqs

    biases = (modulator_bias, projector_bias, combiner_bias, expander_bias, reducer_bias)
    packed = lax.all_gather(jnp.concatenate(biases), "group", axis=0)
    start = 0
    full_biases = []
    for bias in biases:
        full_biases.append(packed[:, start : start + bias.size].reshape(-1).astype(F32))
        start += bias.size
    mod_bias, proj_bias, comb_bias, exp_bias, red_bias = full_biases
    all_condition = lax.all_gather(condition, ("group", "replica"), axis=0)
    all_silu = jax.nn.silu(all_condition.astype(F32)).astype(LOW)
    own_silu = lax.dynamic_slice_in_dim(all_silu, group * rows, rows, 2)
    peer_silu = pick(own_silu.reshape(groups, replicas, latents, rows), rep, 1)
    mod_part = contract(peer_silu.reshape(groups * latents, rows), modulator, 1, 0)
    modulation = lax.psum_scatter(mod_part, "group", scatter_dimension=0, tiled=True) + mod_bias
    pieces = [
        modulation[:, None, position * model : (position + 1) * model] for position in range(6)
    ]
    shift_attn, scale_attn, gate_attn, shift_mlp, scale_mlp, gate_mlp = pieces

    full_projector = lax.all_gather(projector, "group", axis=0, tiled=True)
    full_combiner = lax.all_gather(combiner, "group", axis=0, tiled=True)
    full_expander = lax.all_gather(expander, "group", axis=0, tiled=True)
    full_reducer = lax.all_gather(reducer, "group", axis=0, tiled=True)

    residual = features.astype(F32)
    normed_one, inverse_one = normalize(residual)
    attn_in = (normed_one * (1.0 + scale_attn) + shift_attn).astype(LOW)
    qkv_bias = jnp.concatenate([proj_bias[:model], jnp.zeros((model,), F32), proj_bias[model:]])

    saved = []
    context_parts = []
    for latent in range(latents):
        qkv = contract(full_projector, attn_in[latent], 0, 1) + qkv_bias[:, None]
        qkv = qkv.astype(LOW).reshape(3, seqs, heads, HEAD_DIM, width)
        tokens = exchange([pick(qkv, seq ^ k, 1) for k in range(seqs)], seqs)
        context, exponent, inverse = attend(tokens)
        saved.append((tokens, context, exponent, inverse))
        mine = put(exchange([context[k] for k in range(seqs)], seqs), seq)
        context_parts.append(mine.reshape(model, width))
    context_low = jnp.stack(context_parts)

    attn_out = (
        jnp.einsum("bet,ef->btf", context_low, full_combiner, preferred_element_type=F32)
        + comb_bias
    )
    hidden = residual + gate_attn * attn_out
    normed_two, inverse_two = normalize(hidden)
    mlp_in = (normed_two * (1.0 + scale_mlp) + shift_mlp).astype(LOW)
    expanded = matmul(mlp_in, full_expander) + exp_bias
    activated = jax.nn.gelu(expanded, approximate=True).astype(LOW)
    reduced = matmul(activated, full_reducer) + red_bias
    block_output = (hidden + gate_mlp * reduced).astype(LOW)

    upstream = cotangent.astype(F32)
    reduced_grad = (gate_mlp * upstream).astype(LOW)
    gate_mlp_grad = jnp.sum(upstream * reduced, 1)
    reducer_total = reduce_shards(outer_sum(activated, reduced_grad), sizes)
    reducer_bias_grad = jnp.sum(reduced_grad.astype(F32), (0, 1))
    activated_grad = matmul_back(reduced_grad, full_reducer)
    _, gelu_back = jax.vjp(partial(jax.nn.gelu, approximate=True), expanded)
    expanded_grad = gelu_back(activated_grad)[0].astype(LOW)
    expander_total = reduce_shards(outer_sum(mlp_in, expanded_grad), sizes)
    expander_bias_grad = jnp.sum(expanded_grad.astype(F32), (0, 1))
    mlp_in_grad = matmul_back(expanded_grad, full_expander)
    scale_mlp_grad = jnp.sum(mlp_in_grad * normed_two, 1)
    shift_mlp_grad = jnp.sum(mlp_in_grad, 1)
    hidden_grad = upstream + normalize_back(
        mlp_in_grad * (1.0 + scale_mlp), normed_two, inverse_two
    )
    attn_out_grad = (gate_attn * hidden_grad).astype(LOW)
    gate_attn_grad = jnp.sum(hidden_grad * attn_out, 1)
    combiner_total = reduce_shards(
        jnp.einsum("bdt,bte->de", context_low, attn_out_grad, preferred_element_type=F32), sizes
    )
    combiner_bias_grad = jnp.sum(attn_out_grad.astype(F32), (0, 1))

    grad_parts = []
    for latent in range(latents):
        context_grad = contract(full_combiner, attn_out_grad[latent], 1, 1).astype(LOW)
        context_grad = context_grad.reshape(seqs, heads, HEAD_DIM, width)
        grads = exchange([pick(context_grad, seq ^ k) for k in range(seqs)], seqs)
        tokens, context, exponent, inverse = saved[latent]
        back = attend_back(tokens, grads, context, exponent, inverse)
        mine = put(exchange([back[k] for k in range(seqs)], seqs), seq)
        grad_parts.append(mine.transpose(1, 0, 2, 3, 4).reshape(3 * model, width))
    qkv_grad = jnp.stack(grad_parts)

    projector_total = reduce_shards(
        jnp.einsum("btd,bet->de", attn_in, qkv_grad, preferred_element_type=F32), sizes
    )
    qkv_sums = jnp.sum(qkv_grad.astype(F32), (0, 2))
    projector_bias_grad = jnp.concatenate([qkv_sums[:model], qkv_sums[2 * model :]])
    attn_in_grad = jnp.einsum(
        "bet,de->btd", qkv_grad, full_projector, preferred_element_type=F32
    )
    scale_attn_grad = jnp.sum(attn_in_grad * normed_one, 1)
    shift_attn_grad = jnp.sum(attn_in_grad, 1)
    features_grad = hidden_grad + normalize_back(
        attn_in_grad * (1.0 + scale_attn), normed_one, inverse_one
    )

    partial_mod = jnp.concatenate(
        [
            shift_attn_grad,
            scale_attn_grad,
            gate_attn_grad,
            shift_mlp_grad,
            scale_mlp_grad,
            gate_mlp_grad,
        ],
        -1,
    )
    modulation_grad = lax.psum(partial_mod, "seq").astype(LOW)
    all_mod = lax.all_gather(modulation_grad, ("group", "replica"), axis=0)
    peer_mod = pick(all_mod.reshape(groups, replicas, latents, -1), rep, 1)
    silu_part = contract(peer_mod.reshape(groups * latents, -1), modulator, 1, 1)
    silu_parts = lax.all_gather(silu_part, "group", axis=0)
    silu_own = lax.dynamic_slice_in_dim(silu_parts, group * latents, latents, 1)
    silu_grad = silu_own.transpose(1, 0, 2).reshape(latents, model)
    _, silu_back = jax.vjp(jax.nn.silu, condition.astype(F32))
    condition_grad = silu_back(silu_grad)[0]
    flat_mod = all_mod.reshape(-1, all_mod.shape[-1])
    modulator_grad = contract(own_silu.reshape(-1, rows), flat_mod, 0, 0)
    mod_sum = jnp.sum(flat_mod.astype(F32), 0)
    modulator_bias_grad = lax.dynamic_slice_in_dim(
        mod_sum, group * modulator_bias.size, modulator_bias.size, 0
    )
    bias_grads = (
        projector_bias_grad,
        combiner_bias_grad,
        expander_bias_grad,
        reducer_bias_grad,
    )
    bias_sum = lax.psum(
        jnp.concatenate(bias_grads).astype(LOW).astype(F32), ("group", "replica", "seq")
    )
    bias_out = []
    start = 0
    for grad in bias_grads:
        size = grad.size // groups
        bias_out.append(lax.dynamic_slice_in_dim(bias_sum, start + group * size, size, 0))
        start += grad.size
    return (
        block_output,
        features_grad,
        condition_grad,
        modulator_grad,
        modulator_bias_grad,
        projector_total,
        bias_out[0],
        combiner_total,
        bias_out[1],
        expander_total,
        bias_out[2],
        reducer_total,
        bias_out[3],
    )


def solution(mesh):
    sizes = (mesh.shape["group"], mesh.shape["replica"], mesh.shape["seq"])
    tokens = P(("group", "replica"), "seq", None)
    matrix, vector = P("group", None), P("group")
    return jax.shard_map(
        partial(body, sizes),
        mesh=mesh,
        in_specs=(tokens, P(("group", "replica"), None)) + (matrix, vector) * 5 + (tokens,),
        out_specs=(tokens, tokens, P(("group", "replica"), None)) + (matrix, vector) * 5,
        check_vma=False,
    )
```

```python
from functools import partial

import jax
import jax.numpy as jnp
from jax import lax
from jax.experimental import pallas as pl
from jax.experimental.pallas import tpu as pltpu
from jax.sharding import PartitionSpec as P

HEADS = 16
HEAD_DIM = 72
SCALE = HEAD_DIM**-0.5
LOW = jnp.bfloat16
F32 = jnp.float32


def contract(left, right, left_dim, right_dim):
    return lax.dot_general(
        left, right, (((left_dim,), (right_dim,)), ((), ())), preferred_element_type=F32
    )


def attend_kernel(count, width, *refs):
    pieces = refs[:count]
    context_ref, exp_ref, inverse_ref = refs[count : count + 3]
    keys, values = refs[count + 3 :]
    step = pl.program_id(1)

    @pl.when(step == 0)
    def _():
        for piece in range(count):
            span = slice(piece * width, (piece + 1) * width)
            keys[span, :] = pieces[piece][1, 0].T
            values[:, span] = pieces[piece][2, 0]

    def one(piece):
        scores = contract(keys[...], pieces[piece][0, 0], 1, 0) * F32(SCALE)
        exponent = jnp.exp(scores - jnp.max(scores, 0, keepdims=True))
        inverse = 1.0 / jnp.sum(exponent, 0, keepdims=True)
        low = exponent.astype(LOW)
        context = contract(values[...], low, 1, 0)
        context_ref[0, 0] = (context * inverse).astype(LOW)
        inverse_ref[0, 0] = inverse
        exp_ref[0, 0] = low

    for piece in range(count):
        pl.when(step == piece)(partial(one, piece))


def attend(pieces):
    count = len(pieces)
    _, heads, dim, width = pieces[0].shape
    total = count * width
    return pl.pallas_call(
        partial(attend_kernel, count, width),
        grid=(heads, count),
        in_specs=[pl.BlockSpec((3, 1, dim, width), lambda h, j: (0, h, 0, 0))] * count,
        out_specs=[
            pl.BlockSpec((1, 1, dim, width), lambda h, j: (j, h, 0, 0)),
            pl.BlockSpec((1, 1, total, width), lambda h, j: (h, j, 0, 0)),
            pl.BlockSpec((1, 1, 1, width), lambda h, j: (h, j, 0, 0)),
        ],
        out_shape=[
            jax.ShapeDtypeStruct((count, heads, dim, width), LOW),
            jax.ShapeDtypeStruct((heads, count, total, width), LOW),
            jax.ShapeDtypeStruct((heads, count, 1, width), F32),
        ],
        scratch_shapes=[pltpu.VMEM((total, dim), LOW), pltpu.VMEM((dim, total), LOW)],
        compiler_params=pltpu.CompilerParams(vmem_limit_bytes=48 << 20),
        cost_estimate=pl.CostEstimate(
            flops=heads * total * total * 1000, transcendentals=0, bytes_accessed=heads * total * total * 2
        ),
        name="attend",
    )(*pieces)


KEY_SPAN = 1024


def attend_back_kernel(count, width, *refs):
    pieces = refs[:count]
    grads = refs[count : 2 * count]
    context_ref, exp_ref, inverse_ref, out_ref = refs[2 * count : 2 * count + 4]
    values, keys, key_sum, value_sum = refs[2 * count + 4 :]
    step = pl.program_id(1)
    total = count * width

    @pl.when(step == 0)
    def _():
        for piece in range(count):
            span = slice(piece * width, (piece + 1) * width)
            values[span, :] = pieces[piece][2, 0].T
            keys[:, span] = pieces[piece][1, 0]
        key_sum[...] = jnp.zeros_like(key_sum)
        value_sum[...] = jnp.zeros_like(value_sum)

    def one(piece):
        query = pieces[piece][0, 0]
        grad = (grads[piece][0].astype(F32) * inverse_ref[0, 0]).astype(LOW)
        row_dot = jnp.sum(grad.astype(F32) * context_ref[0, 0].astype(F32), 0, keepdims=True)
        query_grad = jnp.zeros(query.shape, F32)
        for start in range(0, total, KEY_SPAN):
            span = slice(start, start + KEY_SPAN)
            exponent = exp_ref[0, 0, span, :]
            probs_grad = contract(values[span, :], grad, 1, 0)
            scores_grad = (exponent.astype(F32) * (probs_grad - row_dot)).astype(LOW)
            query_grad += contract(keys[:, span], scores_grad, 1, 0)
            value_sum[:, span] += contract(grad, exponent, 1, 1)
            key_sum[:, span] += contract(query, scores_grad, 1, 1)
        out_ref[piece, 0, 0] = (query_grad * F32(SCALE)).astype(LOW)

    for piece in range(count):
        pl.when(step == piece)(partial(one, piece))

    @pl.when(step == count - 1)
    def _():
        for piece in range(count):
            span = slice(piece * width, (piece + 1) * width)
            out_ref[piece, 1, 0] = (key_sum[:, span] * F32(SCALE)).astype(LOW)
            out_ref[piece, 2, 0] = value_sum[:, span].astype(LOW)


def attend_back(pieces, grads, context, exponent, inverse):
    count = len(pieces)
    _, heads, dim, width = pieces[0].shape
    total = count * width
    return pl.pallas_call(
        partial(attend_back_kernel, count, width),
        grid=(heads, count),
        in_specs=[pl.BlockSpec((3, 1, dim, width), lambda h, j: (0, h, 0, 0))] * count
        + [pl.BlockSpec((1, dim, width), lambda h, j: (h, 0, 0))] * count
        + [
            pl.BlockSpec((1, 1, dim, width), lambda h, j: (j, h, 0, 0)),
            pl.BlockSpec((1, 1, total, width), lambda h, j: (h, j, 0, 0)),
            pl.BlockSpec((1, 1, 1, width), lambda h, j: (h, j, 0, 0)),
        ],
        out_specs=pl.BlockSpec((count, 3, 1, dim, width), lambda h, j: (0, 0, h, 0, 0)),
        out_shape=jax.ShapeDtypeStruct((count, 3, heads, dim, width), LOW),
        scratch_shapes=[
            pltpu.VMEM((total, dim), LOW),
            pltpu.VMEM((dim, total), LOW),
            pltpu.VMEM((dim, total), F32),
            pltpu.VMEM((dim, total), F32),
        ],
        compiler_params=pltpu.CompilerParams(vmem_limit_bytes=48 << 20),
        cost_estimate=pl.CostEstimate(
            flops=heads * total * total * 1000, transcendentals=0, bytes_accessed=heads * total * total * 2
        ),
        name="attend_back",
    )(*pieces, *grads, context, exponent, inverse)


def swap(value, axis, size, distance):
    return lax.ppermute(value, axis, [(index, index ^ distance) for index in range(size)])


def pick(array, index, axis=0):
    return lax.dynamic_index_in_dim(array, index, axis, keepdims=False)


def weave(bit, mine, other):
    return jnp.where(
        bit == 0, jnp.concatenate([mine, other]), jnp.concatenate([other, mine])
    )


def copy_all(pairs, semaphores):
    copies = [
        pltpu.make_async_copy(source, target, semaphores.at[number])
        for number, (source, target) in enumerate(pairs)
    ]
    for copy in copies:
        copy.start()
    for copy in copies:
        copy.wait()


def place_kernel(sets, count, lead, *refs):
    out, semaphores = refs[-2:]
    me = lax.axis_index("seq")
    where = [
        out.at[(slice(None),) * lead + (s, me ^ k)] for s in range(sets) for k in range(count)
    ]
    copy_all(list(zip(refs[:-2], where)), semaphores)


def place(sets, lead):
    parts = [part for pieces in sets for part in pieces]
    count = len(sets[0])
    shape = parts[0].shape
    out = shape[:lead] + (len(sets), count) + shape[lead:]
    hbm = pl.BlockSpec(memory_space=pl.ANY)
    return pl.pallas_call(
        partial(place_kernel, len(sets), count, lead),
        in_specs=[hbm] * len(parts),
        out_specs=pl.BlockSpec(memory_space=pltpu.VMEM),
        out_shape=jax.ShapeDtypeStruct(out, parts[0].dtype),
        scratch_shapes=[pltpu.SemaphoreType.DMA((len(parts),))],
        name="place",
    )(*parts)


def deal_kernel(sets, count, lead, source, *refs):
    outs, semaphores = refs[:-1], refs[-1]
    me = lax.axis_index("seq")
    where = [
        source.at[(slice(None),) * lead + (s, me ^ k)] for s in range(sets) for k in range(count)
    ]
    copy_all(list(zip(where, outs)), semaphores)


def deal(source, lead):
    shape = source.shape
    sets, count = shape[lead : lead + 2]
    block = jax.ShapeDtypeStruct(shape[:lead] + shape[lead + 2 :], source.dtype)
    hbm = pl.BlockSpec(memory_space=pl.ANY)
    outs = pl.pallas_call(
        partial(deal_kernel, sets, count, lead),
        in_specs=[pl.BlockSpec(memory_space=pltpu.VMEM)],
        out_specs=[hbm] * (sets * count),
        out_shape=[block] * (sets * count),
        scratch_shapes=[pltpu.SemaphoreType.DMA((sets * count,))],
        name="deal",
    )(source)
    return [outs[s * count : (s + 1) * count] for s in range(sets)]


def exchange(chunks, size):
    return [chunks[0]] + [swap(chunks[k], "seq", size, k) for k in range(1, size)]


def add_low(one, other):
    return (one.astype(F32) + other.astype(F32)).astype(LOW)


def tie(values, others):
    return lax.optimization_barrier((values, others))[0]


class Order:
    def __init__(self):
        self.last = ()

    def __call__(self, step, *inputs):
        result = step(*tie(inputs, self.last))
        self.last = result
        return result


PAIRS = [[0, 1], [2, 3]]


class Reduction:
    def __init__(self, order, grad, fast, vector=None):
        self.order, self.fast = order, fast
        self.rows, self.cols = grad.shape
        self.grad = grad
        self.vector = vector
        seq, rep = lax.axis_index("seq"), lax.axis_index("replica")
        self.near, self.group, self.far, self.low = (
            seq & 1, lax.axis_index("group"), seq >> 1, rep & 1,
        )
        if self.fast:
            view = self.grad.reshape(2, self.rows // 2, self.cols)
            self.value = lax.psum_scatter(
                view, "seq", scatter_dimension=1, axis_index_groups=PAIRS, tiled=True
            )
            self.came = None
            self.vector_came = None if vector is None else swap(vector, "seq", 4, 1)

    def pass_on(self, how, work):
        if not self.fast:
            return
        state = (self.value, self.came, self.vector, self.vector_came)

        def step(value, came, vector, vector_came):
            if vector_came is not None:
                vector = vector + vector_came
            return work(value, came), vector

        (sent, kept), self.vector = self.order(step, *state)
        self.value, self.came = kept, swap(sent, *how)
        self.vector_came = None
        if self.summing and self.vector is not None:
            self.vector_came = swap(self.vector, *how)

    def halve(self, how, bit):
        self.summing = True

        def work(value, came):
            if came is None:
                part = lambda index: pick(value, index)
            else:
                shape = (2, value.shape[0] // 2, self.cols)
                value, came = value.reshape(shape), came.reshape(shape)
                part = lambda index: add_low(pick(value, index), pick(came, index))
            return part(1 - bit), part(bit)

        self.pass_on(how, work)

    def y(self):
        self.halve(("group", 2, 1), self.group)

    def x(self):
        self.halve(("seq", 4, 2), self.far)

    def z(self):
        self.halve(("replica", 4, 1), self.low)

    def zz(self):
        self.pass_on(("replica", 4, 2), lambda value, came: (add_low(value, came),) * 2)

    def back_z(self):
        self.summing = False
        self.pass_on(("replica", 4, 1), lambda value, came: (add_low(value, came),) * 2)

    def back_x(self):
        self.pass_on(("seq", 4, 2), lambda value, came: (weave(self.low, value, came),) * 2)

    def back_core(self):
        self.pass_on(("seq", 4, 1), lambda value, came: (weave(self.far, value, came),) * 2)

    def result(self):
        if not self.fast:
            part = lax.psum_scatter(self.grad, "group", scatter_dimension=0, tiled=True)
            if self.vector is not None:
                self.vector = lax.psum(self.vector, ("group", "replica", "seq"))
            return lax.psum(part, ("replica", "seq")).astype(F32)
        return weave(self.near, self.value, self.came).astype(F32)


def normalize(values):
    centre = jnp.mean(values, -1, keepdims=True)
    centred = values - centre
    inverse = lax.rsqrt(jnp.mean(centred * centred, -1, keepdims=True) + 1e-06)
    return (centred * inverse, inverse)


def normalize_back(grad_in, normed, inverse):
    return (
        grad_in
        - jnp.mean(grad_in, -1, keepdims=True)
        - normed * jnp.mean(grad_in * normed, -1, keepdims=True)
    ) * inverse


def matmul(operand, matrix):
    return jnp.einsum("btd,de->bte", operand, matrix, preferred_element_type=F32)


def matmul_back(operand, matrix):
    return jnp.einsum("bte,de->btd", operand, matrix, preferred_element_type=F32)


def outer_sum(operand, other):
    return jnp.einsum("btd,bte->de", operand, other, preferred_element_type=F32)


def body(
    sizes,
    features,
    condition,
    modulator,
    modulator_bias,
    projector,
    projector_bias,
    combiner,
    combiner_bias,
    expander,
    expander_bias,
    reducer,
    reducer_bias,
    cotangent,
):
    groups, replicas, seqs = sizes
    group = lax.axis_index("group")
    rep = lax.axis_index("replica")
    seq = lax.axis_index("seq")
    latents, width, model = features.shape
    rows = modulator.shape[0]

    fast = sizes == (2, 4, 4)
    order = Order()
    near, half = seq & 1, rows // 2
    other = (1 - group) * rows
    silu_low = jax.nn.silu(condition.astype(F32)).astype(LOW)
    biases = (modulator_bias, projector_bias, combiner_bias, expander_bias, reducer_bias)
    packed = jnp.concatenate(biases)

    if fast:
        first = lax.dynamic_slice_in_dim(projector, near * half, half, 0)
        silu_low, packed, first = order(lambda *values: values, silu_low, packed, first)
        other_silu, other_packed = swap((silu_low, packed), "group", 2, 1)
        first = swap(first, "group", 2, 1)
        sides = lax.dynamic_slice_in_dim(
            jnp.concatenate([silu_low, other_silu]), group * rows, rows, 1
        )
        mod_part = contract(sides, modulator, 1, 0)
        modulation = mod_part[:latents] + swap(mod_part[latents:], "group", 2, 1)
        both = jnp.where(
            group == 0, jnp.stack([packed, other_packed]), jnp.stack([other_packed, packed])
        )
    else:
        both = lax.all_gather(packed, "group", axis=0)
        sides = lax.all_gather(silu_low, "group", axis=0).reshape(groups * latents, model)
        sides = lax.dynamic_slice_in_dim(sides, group * rows, rows, 1)
        mod_part = contract(sides, modulator, 1, 0)
        modulation = lax.psum_scatter(mod_part, "group", scatter_dimension=0, tiled=True)
    start = 0
    full_biases = []
    for bias in biases:
        full_biases.append(both[:, start : start + bias.size].reshape(-1).astype(F32))
        start += bias.size
    mod_bias, proj_bias, comb_bias, exp_bias, red_bias = full_biases
    modulation = modulation + mod_bias
    pieces = [
        modulation[:, None, position * model : (position + 1) * model] for position in range(6)
    ]
    shift_attn, scale_attn, gate_attn, shift_mlp, scale_mlp, gate_mlp = pieces

    residual = features.astype(F32)
    normed_one, inverse_one = normalize(residual)
    attn_in = (normed_one * (1.0 + scale_attn) + shift_attn).astype(LOW)
    qkv_bias = jnp.concatenate([proj_bias[:model], jnp.zeros((model,), F32), proj_bias[model:]])

    def insert(full, part, position):
        return lax.dynamic_update_slice_in_dim(full, part, position, 0)

    if fast:
        full_projector = jnp.concatenate([projector, projector])
        attn_in, full_projector = order(lambda *values: values, attn_in, full_projector)
        first = order(lambda value: value, first)
        second = swap(first, "seq", 4, 1)
        big = reducer.shape[0]
        red_first = lax.dynamic_slice_in_dim(reducer, near * (big // 2), big // 2, 0)
        early_combiner, early_expander, red_first = tie((combiner, expander, red_first), first)
        red_first = swap(red_first, "group", 2, 1)
        full_combiner = lax.all_gather(early_combiner, "group", axis=0, tiled=True)
        full_expander = lax.all_gather(early_expander, "group", axis=0, tiled=True)
        full_projector = insert(full_projector, first, other + near * half)
        full_projector = order(
            lambda full, part: insert(full, part, other + (1 - near) * half),
            full_projector,
            second,
        )
    else:
        full_projector, full_combiner, full_expander, full_reducer = [
            lax.all_gather(shard, "group", axis=0, tiled=True)
            for shard in (projector, combiner, expander, reducer)
        ]

    heads = HEADS // seqs // 2
    units = [(latent, part) for latent in range(latents) for part in range(2)]

    def project(tokens):
        qkv = contract(full_projector, tokens, 0, 1) + qkv_bias[:, None]
        qkv = qkv.astype(LOW).reshape(3, 2, seqs, heads, HEAD_DIM, width)
        return deal(qkv, 1)

    sends = {}
    sends[0, 0], sends[0, 1] = order(project, attn_in[0])
    tokens = exchange(sends[0, 0], seqs)
    for latent in range(1, latents):
        sends[latent, 0], sends[latent, 1] = order(project, attn_in[latent])
    saved = {}
    contexts = {}
    for number, unit in enumerate(units):
        tokens = order(lambda value: value, tokens)
        if number + 1 < len(units):
            chunk = order(lambda value: value, sends[units[number + 1]])
            ahead = exchange(chunk, seqs)
        context, exponent, inverse = order(attend, tokens)
        saved[unit] = (tokens, context, exponent, inverse)
        contexts[unit] = exchange([context[k] for k in range(seqs)], seqs)
        tokens = ahead
        if number == 2 and fast:
            red_first = order(lambda value: value, red_first)
            red_second = swap(red_first, "seq", 4, 1)
    if fast:
        far_rows = (1 - group) * big
        full_reducer = order(lambda value: jnp.concatenate([value, value]), reducer)
        full_reducer = order(
            lambda full, one, two: insert(
                insert(full, one, far_rows + near * (big // 2)),
                two,
                far_rows + (1 - near) * (big // 2),
            ),
            full_reducer,
            red_first,
            red_second,
        )

    def gather_context(*parts):
        return jnp.stack(
            [
                place(parts[2 * latent : 2 * latent + 2], 0).reshape(model, width)
                for latent in range(latents)
            ]
        )

    context_low = order(gather_context, *[contexts[unit] for unit in units])
    attn_out = (
        jnp.einsum("bet,ef->btf", context_low, full_combiner, preferred_element_type=F32)
        + comb_bias
    )
    hidden = residual + gate_attn * attn_out
    normed_two, inverse_two = normalize(hidden)
    mlp_in = (normed_two * (1.0 + scale_mlp) + shift_mlp).astype(LOW)
    expanded = matmul(mlp_in, full_expander) + exp_bias
    activated = jax.nn.gelu(expanded, approximate=True).astype(LOW)

    upstream = cotangent.astype(F32)
    reduced_grad = (gate_mlp * upstream).astype(LOW)
    reducer_bias_grad = jnp.sum(reduced_grad.astype(F32), (0, 1))

    def weight_grad(form):
        return lambda one, two: jnp.einsum(form, one, two, preferred_element_type=F32).astype(LOW)

    red = Reduction(order, order(weight_grad("btd,bte->de"), activated, reduced_grad), fast)

    def through_gelu(grad, value):
        _, gelu_back = jax.vjp(partial(jax.nn.gelu, approximate=True), value)
        low = gelu_back(matmul_back(grad, full_reducer))[0].astype(LOW)
        return low, jnp.sum(low.astype(F32), (0, 1))

    expanded_grad, expander_bias_grad = order(through_gelu, reduced_grad, expanded)
    exp = Reduction(order, order(weight_grad("btd,bte->de"), mlp_in, expanded_grad), fast)
    red.y()

    def through_expander(grad):
        mlp_in_grad = matmul_back(grad, full_expander)
        scale_mlp_grad = jnp.sum(mlp_in_grad * normed_two, 1)
        shift_mlp_grad = jnp.sum(mlp_in_grad, 1)
        hidden_grad = upstream + normalize_back(
            mlp_in_grad * (1.0 + scale_mlp), normed_two, inverse_two
        )
        attn_out_grad = (gate_attn * hidden_grad).astype(LOW)
        gate_attn_grad = jnp.sum(hidden_grad * attn_out, 1)
        sums = jnp.sum(attn_out_grad.astype(F32), (0, 1))
        early = jnp.concatenate([gate_attn_grad, shift_mlp_grad, scale_mlp_grad], -1)
        return hidden_grad, attn_out_grad, sums, early

    hidden_grad, attn_out_grad, combiner_bias_grad, early_mod = order(
        through_expander, expanded_grad
    )

    def through_combiner(grad):
        low = contract(full_combiner, grad, 1, 1).astype(LOW)
        return deal(low.reshape(2, seqs, heads, HEAD_DIM, width), 0)

    grads = {}
    for latent in range(latents):
        dealt = order(through_combiner, attn_out_grad[latent])
        for part, chunk in enumerate(dealt):
            grads[latent, part] = exchange(chunk, seqs)
    bias_vector = jnp.concatenate([combiner_bias_grad, expander_bias_grad, reducer_bias_grad])
    comb = Reduction(
        order, order(weight_grad("bdt,bte->de"), context_low, attn_out_grad), fast, bias_vector
    )
    if fast:
        early_came = swap(early_mod, "seq", 4, 1)
    exp.y()

    def project_part(parts):
        grad = jnp.stack([place([pieces], 1).reshape(-1, width) for pieces in parts])
        sums = jnp.sum(grad.astype(F32), (0, 2))
        third = sums.size // 3
        total = weight_grad("btd,bet->de")(attn_in, grad)
        return grad, total, jnp.concatenate([sums[:third], sums[2 * third :]])

    received = {}
    for number, unit in enumerate([(0, 0), (1, 0), (0, 1), (1, 1)]):
        tokens, context, exponent, inverse = saved[unit]
        back = order(attend_back, tokens, grads[unit], context, exponent, inverse)
        received[unit] = exchange([back[k] for k in range(seqs)], seqs)
        if number == 0:
            red.x()
            if fast:
                early_mod = order(jnp.add, early_mod, early_came)
                early_came = swap(early_mod, "seq", 4, 2)
        if number == 1:
            comb.y()
        if number == 2:
            qkv_grad_one, proj_grad, vector = order(
                project_part, [received[0, 0], received[1, 0]]
            )
            proj_one = Reduction(order, proj_grad, fast, vector)
    proj_one.y()
    red.z()
    exp.x()
    comb.x()

    def finish(value):
        reduced = matmul(value, full_reducer) + red_bias
        return (hidden + gate_mlp * reduced).astype(LOW), jnp.sum(upstream * reduced, 1)

    block_output, gate_mlp_grad = order(finish, activated)
    qkv_grad_two, proj_grad, vector = order(project_part, [received[0, 1], received[1, 1]])
    proj_two = Reduction(order, proj_grad, fast, vector)
    red.zz()
    proj_one.x()
    third = qkv_grad_one.shape[1] // 3

    def through_projector(one, two):
        qkv_grad = jnp.concatenate(
            [
                grad[:, index * third : (index + 1) * third]
                for index in range(3)
                for grad in (one, two)
            ],
            1,
        )
        attn_in_grad = jnp.einsum(
            "bet,de->btd", qkv_grad, full_projector, preferred_element_type=F32
        )
        scale_attn_grad = jnp.sum(attn_in_grad * normed_one, 1)
        shift_attn_grad = jnp.sum(attn_in_grad, 1)
        features_grad = hidden_grad + normalize_back(
            attn_in_grad * (1.0 + scale_attn), normed_one, inverse_one
        )
        return features_grad, jnp.concatenate([shift_attn_grad, scale_attn_grad], -1)

    features_grad, late_mod = order(through_projector, qkv_grad_one, qkv_grad_two)
    late_mod = jnp.concatenate([late_mod, gate_mlp_grad], -1)
    proj_two.y()
    red.back_z()
    exp.z()
    comb.z()
    proj_one.z()
    if fast:
        late_came = swap(late_mod, "seq", 4, 1)
        early_mod = early_mod + early_came
        late_mod = order(jnp.add, late_mod, late_came)
        late_came = swap(late_mod, "seq", 4, 2)
    else:
        early_mod, late_mod = lax.psum((early_mod, late_mod), "seq")
    red.back_x()
    exp.zz()
    comb.zz()
    proj_two.x()
    proj_one.zz()
    if fast:
        late_mod = order(jnp.add, late_mod, late_came)

    modulation_grad = jnp.concatenate(
        [late_mod[:, : 2 * model], early_mod, late_mod[:, 2 * model :]], -1
    ).astype(LOW)
    own_mod = jnp.concatenate([modulation_grad, silu_low], -1)

    def silu_grads(mod):
        return contract(mod[:, : 6 * model], modulator, 1, 1)

    if fast:
        came = swap(own_mod, "replica", 4, 1)
        peer_came = swap(own_mod, "group", 2, 1)
        exp.back_z()
        comb.back_z()
        red.back_core()
        own_mod, peer_mod = order(
            lambda one, two, three: (weave(rep & 1, one, two), jnp.concatenate([one, three])),
            own_mod,
            came,
            peer_came,
        )
        came = swap(own_mod, "replica", 4, 2)
        silu_part = order(silu_grads, peer_mod)
        silu_came = swap(silu_part[latents:], "group", 2, 1)
        proj_two.z()
        proj_one.back_z()
        own_mod = order(partial(weave, rep >> 1), own_mod, came)
        came = swap(own_mod, "group", 2, 1)
        exp.back_x()
        comb.back_x()
        proj_two.zz()
        silu_grad = order(
            lambda one, two: jnp.where(
                group == 0, jnp.concatenate([one, two], 1), jnp.concatenate([two, one], 1)
            ),
            silu_part[:latents],
            silu_came,
        )
        flat_mod = order(partial(weave, group), own_mod, came)
    else:
        all_mod = lax.all_gather(own_mod, ("group", "replica"), axis=0)
        flat_mod = all_mod.reshape(-1, all_mod.shape[-1])
        peer_mod = pick(all_mod.reshape(groups, replicas, latents, -1), rep, 1)
        silu_part = silu_grads(peer_mod.reshape(groups * latents, -1))
        silu_parts = lax.all_gather(silu_part, "group", axis=0)
        silu_own = lax.dynamic_slice_in_dim(silu_parts, group * latents, latents, 1)
        silu_grad = silu_own.transpose(1, 0, 2).reshape(latents, model)
    _, silu_back = jax.vjp(jax.nn.silu, condition.astype(F32))
    condition_grad = silu_back(silu_grad)[0]

    def modulator_grads(mod):
        own_silu = lax.dynamic_slice_in_dim(mod[:, 6 * model :], group * rows, rows, 1)
        mod = mod[:, : 6 * model]
        sums = jnp.sum(mod.astype(F32), 0)
        size = modulator_bias.size
        return (
            contract(own_silu, mod, 0, 0),
            lax.dynamic_slice_in_dim(sums, group * size, size, 0),
        )

    modulator_grad, modulator_bias_grad = order(modulator_grads, flat_mod)
    proj_one.back_x()
    proj_two.back_z()
    exp.back_core()
    comb.back_core()
    proj_two.back_x()
    proj_one.back_core()
    proj_two.back_core()

    def own_part(vector):
        size = vector.size // groups
        return lax.dynamic_slice_in_dim(vector, group * size, size, 0)

    results = [total.result() for total in (proj_one, proj_two, comb, exp, red)]
    projector_total = jnp.concatenate(
        [
            part[:, index * third : (index + 1) * third]
            for index in range(3)
            for part in results[:2]
        ],
        1,
    )
    sixth = model // 2
    projector_bias_total = jnp.concatenate(
        [
            part[index * sixth : (index + 1) * sixth]
            for index in range(2)
            for part in (proj_one.vector, proj_two.vector)
        ]
    )
    comb_out, exp_out, red_out = jnp.split(comb.vector, [model, model + expander.shape[1]])
    return (
        block_output,
        features_grad,
        condition_grad,
        modulator_grad,
        modulator_bias_grad,
        projector_total,
        own_part(projector_bias_total),
        results[2],
        own_part(comb_out),
        results[3],
        own_part(exp_out),
        results[4],
        own_part(red_out),
    )


def solution(mesh):
    sizes = (mesh.shape["group"], mesh.shape["replica"], mesh.shape["seq"])
    tokens = P(("group", "replica"), "seq", None)
    matrix, vector = P("group", None), P("group")
    return jax.shard_map(
        partial(body, sizes),
        mesh=mesh,
        in_specs=(tokens, P(("group", "replica"), None)) + (matrix, vector) * 5 + (tokens,),
        out_specs=(tokens, tokens, P(("group", "replica"), None)) + (matrix, vector) * 5,
        check_vma=False,
    )
```
